32 devices in a mesh: rows: 16 (over z, y, x), grp: 2 (over core).
Axes of the slice: x: 2, y: 2, z: 4, core: 2. Of those that a mesh axis runs over, the one named last changes fastest.
Arguments:
- start_basis: bfloat16 [16384, 64], P(('rows', 'grp')), may hold values from -6 to 6
- kernel_blocks: bfloat16 [2944, 256, 256], P(('rows', 'grp')), may hold values from -0.0390625 to 0.0390625
- block_row: int32 [2944], P(('rows', 'grp')), may hold values from 0 to 63, as said below
- block_col: int32 [2944], P(('rows', 'grp')), may hold values from 0 to 63, as said below
- block_count: int32 [32], P(('rows', 'grp')), may hold values from 1 to 92, as said below
Outputs:
- embedding: float32 [16384, 64], P(('rows', 'grp'))
- projected: float32 [64, 64], replicated
The draws below stay inside these ranges and needn't reach their ends.
Inputs may be any that keep to these rules, and one draw needn't show every extreme that they name: block_count[d] is the number of live slots of device d, its first ones; device 0 has all 92 live and the last device has 3. `block_row`: each slot's row block is one of its own device's 2 row blocks. `block_col`: each slot's column block is at least its row block; among one device's live slots at most 3 have their column block on any one device, the last device's live slots all lie on itself, and device 0 has a live slot whose column block lies on the last device.
All inputs are finite; a program needn't handle non-finite values.
Results may differ from the reference program's by a relative error of at most 0.0034.
Values may be sent and summed in bfloat16 or wider, within the bound.
A program may use at most 128 MiB of HBM per device.

```python
import jax
import jax.numpy as jnp
from jax import lax

B = 256
C = 64
ITERS = 2
RB_DEV = 2
SLOTS = 92
ROW_BLOCKS = 64
TOTAL_ROWS = 16384
TOTAL_SLOTS = 2944


def layout(key):
    devices = TOTAL_SLOTS // SLOTS
    device_ids = jnp.arange(devices, dtype=jnp.int32)
    base_count = (SLOTS * (devices - device_ids) + devices - 1) // devices
    cut_count = jax.random.randint(jax.random.fold_in(key, 11), (devices,), 0, max(1, SLOTS // 8) + 1)
    cut_count = jnp.where((device_ids == 0) | (device_ids == devices - 1), 0, cut_count)
    live_count = jnp.maximum(base_count - cut_count, 1)
    slot_ids = jnp.arange(SLOTS, dtype=jnp.int32)
    alive_mask = slot_ids[None, :] < live_count[:, None]
    random_keys = jax.random.randint(jax.random.fold_in(key, 12), (devices, SLOTS), 0, 1 << 19)
    scores = (jnp.where(alive_mask, 0, 1 << 20) + random_keys) * SLOTS + slot_ids[None, :]
    sort_order = jnp.argsort(scores, axis=1, stable=True)
    live_rank = jnp.argsort(sort_order, axis=1, stable=True).astype(jnp.int32)
    reach_span = devices - device_ids
    offset = jax.random.randint(jax.random.fold_in(key, 13), (devices,), 0, 1 << 20) % reach_span
    offset = jnp.where(device_ids == 0, devices - 1, offset)
    target_dev = device_ids[:, None] + (live_rank + offset[:, None]) % reach_span[:, None]
    row_local = jax.random.randint(jax.random.fold_in(key, 14), (devices, SLOTS), 0, RB_DEV)
    col_pick = jax.random.randint(jax.random.fold_in(key, 15), (devices, SLOTS), 0, 1 << 20)
    self_target = target_dev == device_ids[:, None]
    col_local = jnp.where(self_target, row_local + col_pick % (RB_DEV - row_local), col_pick % RB_DEV)
    row_ids = device_ids[:, None] * RB_DEV + row_local
    col_ids = target_dev * RB_DEV + col_local
    return (row_ids.reshape(-1).astype(jnp.int32), col_ids.reshape(-1).astype(jnp.int32), live_count.astype(jnp.int32))


def draw_block_row(key, part):
    return layout(key)[0]


def draw_block_col(key, part):
    return layout(key)[1]


def draw_block_count(key, part):
    return layout(key)[2]


def shard_levels(key, extent, shards, smallest, high):
    factor_of = 1.0
    for axis_at, blocks in shards:
        steps = jax.random.uniform(jax.random.fold_in(jax.random.fold_in(key, 6), axis_at), (blocks,), jnp.float32, smallest / len(shards), high / len(shards))
        factor_of = factor_of * jnp.repeat(jnp.exp(steps), extent[axis_at] // blocks).reshape((-1,) + (1,) * (len(extent) - 1 - axis_at))
    return factor_of


def centred(rng, dims, deviation, bound, pieces=(), kind=jnp.bfloat16):
    entries = deviation * jax.random.normal(rng, dims, jnp.float32)
    if pieces:
        entries = entries * shard_levels(rng, dims, pieces, -0.22, 0.18)
    return jnp.clip(entries, -bound, bound).astype(kind)


def setup_inputs(seed: int = 0) -> dict:
    streams_of = jax.random.split(jax.random.key(seed), 6)
    start_basis = centred(streams_of[0], (TOTAL_ROWS, C), 1.0, 6.0, ((0, 32),))
    kernel_blocks = centred(streams_of[1], (TOTAL_SLOTS, B, B), (B * SLOTS) ** -0.5, 0.0390625, ((0, 32),))
    block_row = draw_block_row(jax.random.fold_in(streams_of[5], 71), 0)
    block_col = draw_block_col(jax.random.fold_in(streams_of[5], 71), 0)
    block_count = draw_block_count(jax.random.fold_in(streams_of[5], 71), 0)
    return dict(start_basis=start_basis, kernel_blocks=kernel_blocks, block_row=block_row, block_col=block_col, block_count=block_count)


def image_of(kernel_blocks, block_row, block_col, block_count, basis):
    devices = TOTAL_SLOTS // SLOTS
    basis_tiles = basis.reshape(ROW_BLOCKS, B, C)
    stacked = kernel_blocks.reshape(devices, SLOTS, B, B)
    row_lists = block_row.reshape(devices, SLOTS)
    col_lists = block_col.reshape(devices, SLOTS)

    def visit(running, inputs):
        blocks, row_ids, col_ids, live_total = inputs
        alive_mask = (jnp.arange(SLOTS, dtype=jnp.int32) < live_total).astype(jnp.float32)[:, None, None]
        blocks_wide = blocks.astype(jnp.float32)
        forward = jnp.einsum('sij,sjc->sic', blocks_wide, basis_tiles[col_ids].astype(jnp.float32), precision=lax.Precision.HIGHEST)
        mirrored = jnp.einsum('sji,sjc->sic', blocks_wide, basis_tiles[row_ids].astype(jnp.float32), precision=lax.Precision.HIGHEST).astype(jnp.bfloat16)
        mirrored = lax.optimization_barrier(mirrored).astype(jnp.float32)
        running = running.at[row_ids].add(forward * alive_mask).at[col_ids].add(mirrored * alive_mask)
        return (running, None)
    running, _ = lax.scan(visit, jnp.zeros((ROW_BLOCKS, B, C), jnp.float32), (stacked, row_lists, col_lists, block_count))
    return running.reshape(TOTAL_ROWS, C)

def reference(start_basis, kernel_blocks, block_row, block_col, block_count):
    basis = start_basis
    result = None
    projected = None
    for iteration in range(ITERS):
        image_rows = image_of(kernel_blocks, block_row, block_col, block_count, basis)
        gram_part = jnp.dot(image_rows.T, image_rows, precision=lax.Precision.HIGHEST) / TOTAL_ROWS
        if iteration == ITERS - 1:
            projected = jnp.dot(basis.astype(jnp.float32).T, image_rows, precision=lax.Precision.HIGHEST) / TOTAL_ROWS
        lower_factor = jnp.linalg.cholesky(gram_part)
        inverse = jax.scipy.linalg.solve_triangular(lower_factor, jnp.eye(C, dtype=jnp.float32), lower=True)
        result = jnp.dot(image_rows, inverse.T, precision=lax.Precision.HIGHEST)
        basis = result.astype(jnp.bfloat16)
    return (result, projected)
```

```python
import functools

import jax
import jax.numpy as jnp
from jax import lax
from jax.experimental import pallas as pl
from jax.experimental.pallas import tpu as pltpu
from jax.sharding import PartitionSpec as P

ITERS = 2
MESH = pl.DeviceIdType.MESH
HIGH = lax.Precision.HIGHEST
NARROW = 3
CHUNKS = 4


def orders_of(bits, kinds):
    down = list(range(bits - 1, -1, -1))
    swapped = list(down)
    if bits >= 3:
        swapped[bits - 3], swapped[bits - 2] = swapped[bits - 2], swapped[bits - 3]
    return [down if kind % 2 == 0 else swapped for kind in range(kinds)]


def place_of(device, order):
    return sum(((device // (1 << b)) % 2) * (1 << i) for i, b in enumerate(order))


def split_even(total, parts):
    edges = [total * i // parts for i in range(parts + 1)]
    return list(zip(edges[:-1], edges[1:]))


def nt_dot(a, b, precision=None):
    return lax.dot_general(
        a, b, (((1,), (1,)), ((), ())), preferred_element_type=jnp.float32, precision=precision
    )


def inverse_factor(gram, columns):
    row_id = lax.broadcasted_iota(jnp.int32, (columns, 2 * columns), 0)
    lane_id = lax.broadcasted_iota(jnp.int32, (columns, 2 * columns), 1)
    unit = jnp.where(lane_id == row_id + columns, 1.0, 0.0).astype(jnp.float32)
    work = jnp.where(lane_id < columns, gram, unit)
    for k in range(columns):
        pivot = work[k : k + 1, k : k + 1]
        guess = lax.rsqrt(pivot)
        scale = guess * (1.5 - 0.5 * (pivot * guess) * guess)
        line = work[k : k + 1, :] * scale
        factor = work[:, k : k + 1] * scale
        work = jnp.where(row_id == k, line, jnp.where(row_id > k, work - factor * line, work))
    return work[:, columns:]


def kernel(
    devices, total_rows, per_peer,
    mslot, mrow, mmask, fplace, fmask,
    start_ref, blocks_hbm, embed_ref, proj_ref,
    blocks, own, gathered, partial, narrow_send, narrow_recv, wide_recv, image, line, line_recv,
    load_sem, ag_send, ag_recv, rs_send, rs_recv, ar_send, ar_recv,
):
    bits = devices.bit_length() - 1
    kinds, columns, size = own.shape
    slots = blocks.shape[0]
    wide = wide_recv.shape[0] // kinds
    rows_at = lax.axis_index("rows")
    grp_at = lax.axis_index("grp")
    me = rows_at * 2 + grp_at
    orders = orders_of(bits, kinds)
    places = [place_of(me, order) for order in orders]

    def partner(b):
        other = me + (1 << b) * (1 - 2 * ((me // (1 << b)) % 2))
        return (other // 2, other % 2)

    loads = [
        pltpu.make_async_copy(
            blocks_hbm.at[pl.ds(lo, hi - lo)], blocks.at[pl.ds(lo, hi - lo)], load_sem.at[i]
        )
        for i, (lo, hi) in enumerate(split_even(slots, CHUNKS))
    ]
    for copy in loads:
        copy.start()
    barrier = pltpu.get_barrier_semaphore()
    for b in range(bits):
        pl.semaphore_signal(barrier, inc=1, device_id=partner(b), device_id_type=MESH)
    pl.semaphore_wait(barrier, bits)

    def mirror_for(device, _):
        sums = [jnp.zeros((columns, size), jnp.float32) for _ in range(kinds)]
        for j in range(per_peer):
            at = device * per_peer + j
            product = jnp.dot(
                own[mrow[at]], blocks[mslot[at]], preferred_element_type=jnp.float32
            )
            for kind in range(kinds):
                sums[kind] = sums[kind] + product * mmask[kind, at]
        for kind in range(kinds):
            partial[kind * devices + place_of(device, orders[kind])] = sums[kind]
        return 0

    def forward_for(slot, _):
        product = nt_dot(gathered[fplace[slot]], blocks[slot])
        for kind in range(kinds):
            image[kind] = image[kind] + product * fmask[kind, slot]
        return 0

    for iteration in range(ITERS):
        last = iteration == ITERS - 1
        for kind in range(kinds):
            if iteration == 0:
                own[kind] = start_ref[kind]
            gathered[kind * devices + places[kind]] = own[kind]
        mirror_parts = split_even(devices, bits - 1)
        for k in range(bits):
            copies = []
            for kind in range(kinds):
                base = kind * devices + (places[kind] // (1 << k)) * (1 << k)
                span = gathered.at[pl.ds(base, 1 << k)]
                copies.append(
                    pltpu.make_async_remote_copy(
                        span, span, ag_send.at[kind, k], ag_recv.at[kind, k],
                        device_id=partner(orders[kind][k]), device_id_type=MESH,
                    )
                )
            for copy in copies:
                copy.start()
            if k == 0 and iteration == 0:
                for copy in loads:
                    copy.wait()
            if k > 0:
                lo, hi = mirror_parts[k - 1]
                lax.fori_loop(lo, hi, mirror_for, 0, unroll=2)
            for copy in copies:
                copy.wait()

        image[...] = jnp.zeros_like(image)
        forward_parts = split_even(slots, bits)
        for k in range(bits - 1, -1, -1):
            narrow = k >= bits - NARROW
            count = 1 << k
            copies = []
            keeps = []
            for kind in range(kinds):
                place = places[kind]
                keep = kind * devices + (place // count) * count
                give = (
                    kind * devices
                    + (place // (2 * count)) * (2 * count)
                    + (1 - (place // count) % 2) * count
                )
                keeps.append(keep)
                if narrow:
                    stage = kind * devices + count

                    def stage_one(i, _, stage=stage, give=give):
                        narrow_send[stage + i] = partial[give + i].astype(jnp.bfloat16)
                        return 0

                    lax.fori_loop(0, count, stage_one, 0)
                    source = narrow_send.at[pl.ds(stage, count)]
                    target = narrow_recv.at[pl.ds(stage, count)]
                else:
                    source = partial.at[pl.ds(give, count)]
                    target = wide_recv.at[pl.ds(kind * wide + count, count)]
                copy = pltpu.make_async_remote_copy(
                    source, target, rs_send.at[kind, k], rs_recv.at[kind, k],
                    device_id=partner(orders[kind][k]), device_id_type=MESH,
                )
                copy.start()
                copies.append(copy)
            lo, hi = forward_parts[bits - 1 - k]
            lax.fori_loop(lo, hi, forward_for, 0, unroll=2)
            for kind in range(kinds):
                copies[kind].wait()
                keep = keeps[kind]

                def add_one(i, _, keep=keep, kind=kind, narrow=narrow, count=count):
                    if narrow:
                        more = narrow_recv[kind * devices + count + i].astype(jnp.float32)
                    else:
                        more = wide_recv[kind * wide + count + i]
                    partial[keep + i] = partial[keep + i] + more
                    return 0

                lax.fori_loop(0, count, add_one, 0)

        gram = jnp.zeros((columns, columns), jnp.float32)
        projection = jnp.zeros((columns, columns), jnp.float32)
        for kind in range(kinds):
            rows = image[kind] + partial[kind * devices + places[kind]]
            image[kind] = rows
            gram = gram + nt_dot(rows, rows, HIGH)
            if last:
                projection = projection + nt_dot(own[kind].astype(jnp.float32), rows, HIGH)
        line[0] = jnp.concatenate([gram, projection], axis=1)
        for b in range(bits):
            copy = pltpu.make_async_remote_copy(
                line.at[b], line_recv.at[b], ar_send.at[b], ar_recv.at[b],
                device_id=partner(b), device_id_type=MESH,
            )
            copy.start()
            copy.wait()
            line[b + 1] = line[b] + line_recv[b]
        whole = line[bits] / total_rows
        if last:
            proj_ref[...] = whole[:, columns:]
        inverse = inverse_factor(whole, columns)
        for kind in range(kinds):
            result = jnp.dot(
                inverse, image[kind], precision=HIGH, preferred_element_type=jnp.float32
            )
            if last:
                embed_ref[:, kind * size : (kind + 1) * size] = result
            else:
                own[kind] = result.astype(jnp.bfloat16)


def on_device(start_basis, kernel_blocks, block_row, block_col, block_count):
    devices = lax.axis_size("rows") * lax.axis_size("grp")
    me = lax.axis_index("rows") * lax.axis_size("grp") + lax.axis_index("grp")
    slots, size, _ = kernel_blocks.shape
    own_rows, columns = start_basis.shape
    kinds = own_rows // size
    per_peer = (slots + devices - 1) // devices
    bits = devices.bit_length() - 1
    orders = orders_of(bits, kinds)
    total_rows = own_rows * devices

    positions = jnp.arange(slots, dtype=jnp.int32)
    alive = positions < block_count[0]
    local_row = jnp.clip(block_row - me * kinds, 0, kinds - 1)
    target = block_col // kinds
    target_block = block_col - target * kinds
    earlier = (
        (target[:, None] == target[None, :])
        & alive[None, :]
        & (positions[None, :] < positions[:, None])
    )
    rank = jnp.sum(earlier.astype(jnp.int32), axis=1)
    spot = jnp.where(alive, target * per_peer + rank, -1)
    hit = spot[None, :] == jnp.arange(devices * per_peer, dtype=jnp.int32)[:, None]
    mslot = jnp.sum(jnp.where(hit, positions[None, :], 0), axis=1)
    mrow = jnp.sum(jnp.where(hit, local_row[None, :], 0), axis=1)
    kind_ids = jnp.arange(kinds, dtype=jnp.int32)[:, None]
    mmask = jnp.any(
        hit[None] & (target_block[None, None, :] == kind_ids[:, :, None]), axis=2
    ).astype(jnp.float32)
    fplace = sum(
        jnp.where(target_block == kind, kind * devices + place_of(target, orders[kind]), 0)
        for kind in range(kinds)
    ).astype(jnp.int32)
    fmask = ((local_row[None, :] == kind_ids) & alive[None, :]).astype(jnp.float32)
    start = start_basis.reshape(kinds, size, columns).transpose(0, 2, 1)

    smem = pl.BlockSpec(memory_space=pltpu.SMEM)
    vmem = pl.BlockSpec(memory_space=pltpu.VMEM)
    wide = 1 << max(bits - NARROW, 0)
    embedded, projected = pl.pallas_call(
        functools.partial(kernel, devices, total_rows, per_peer),
        out_shape=(
            jax.ShapeDtypeStruct((columns, own_rows), jnp.float32),
            jax.ShapeDtypeStruct((columns, columns), jnp.float32),
        ),
        in_specs=[smem] * 5 + [vmem, pl.BlockSpec(memory_space=pl.ANY)],
        out_specs=(vmem, vmem),
        scratch_shapes=[
            pltpu.VMEM((slots, size, size), jnp.bfloat16),
            pltpu.VMEM((kinds, columns, size), jnp.bfloat16),
            pltpu.VMEM((kinds * devices, columns, size), jnp.bfloat16),
            pltpu.VMEM((kinds * devices, columns, size), jnp.float32),
            pltpu.VMEM((kinds * devices, columns, size), jnp.bfloat16),
            pltpu.VMEM((kinds * devices, columns, size), jnp.bfloat16),
            pltpu.VMEM((kinds * wide, columns, size), jnp.float32),
            pltpu.VMEM((kinds, columns, size), jnp.float32),
            pltpu.VMEM((bits + 1, columns, 2 * columns), jnp.float32),
            pltpu.VMEM((bits, columns, 2 * columns), jnp.float32),
            pltpu.SemaphoreType.DMA((CHUNKS,)),
            pltpu.SemaphoreType.DMA((kinds, bits)),
            pltpu.SemaphoreType.DMA((kinds, bits)),
            pltpu.SemaphoreType.DMA((kinds, bits)),
            pltpu.SemaphoreType.DMA((kinds, bits)),
            pltpu.SemaphoreType.DMA((bits,)),
            pltpu.SemaphoreType.DMA((bits,)),
        ],
        compiler_params=pltpu.CompilerParams(
            collective_id=0, has_side_effects=True, vmem_limit_bytes=62 * 1024 * 1024
        ),
    )(mslot, mrow, mmask, fplace, fmask, start, kernel_blocks)
    return embedded.T, projected


def solution(mesh):
    in_specs = (
        P(("rows", "grp"), None),
        P(("rows", "grp"), None, None),
        P(("rows", "grp")),
        P(("rows", "grp")),
        P(("rows", "grp")),
    )
    out_specs = (P(("rows", "grp"), None), P())
    return jax.shard_map(
        on_device, mesh=mesh, in_specs=in_specs, out_specs=out_specs, check_vma=False
    )
```

```python
import functools

import jax
import jax.numpy as jnp
from jax import lax
from jax.experimental import pallas as pl
from jax.experimental.pallas import tpu as pltpu
from jax.sharding import PartitionSpec as P

ITERS = 2
MESH = pl.DeviceIdType.MESH
HIGH = lax.Precision.HIGHEST
NARROW = 3
CHUNKS = 4


def orders_of(bits, kinds):
    down = list(range(bits - 1, -1, -1))
    swapped = list(down)
    if bits >= 3:
        swapped[bits - 3], swapped[bits - 2] = swapped[bits - 2], swapped[bits - 3]
    return [down if kind % 2 == 0 else swapped for kind in range(kinds)]


def place_of(device, order):
    return sum(((device // (1 << b)) % 2) * (1 << i) for i, b in enumerate(order))


def split_even(total, parts):
    edges = [total * i // parts for i in range(parts + 1)]
    return list(zip(edges[:-1], edges[1:]))


def nt_dot(a, b, precision=None):
    return lax.dot_general(
        a, b, (((1,), (1,)), ((), ())), preferred_element_type=jnp.float32, precision=precision
    )


def inverse_factor(gram, columns):
    row_id = lax.broadcasted_iota(jnp.int32, (columns, 2 * columns), 0)
    lane_id = lax.broadcasted_iota(jnp.int32, (columns, 2 * columns), 1)
    unit = jnp.where(lane_id == row_id + columns, 1.0, 0.0).astype(jnp.float32)
    work = jnp.where(lane_id < columns, gram, unit)
    for k in range(columns):
        pivot = work[k : k + 1, k : k + 1]
        guess = lax.rsqrt(pivot)
        scale = guess * (1.5 - 0.5 * (pivot * guess) * guess)
        line = work[k : k + 1, :] * scale
        factor = work[:, k : k + 1] * scale
        work = jnp.where(row_id == k, line, jnp.where(row_id > k, work - factor * line, work))
    return work[:, columns:]


def kernel(
    devices, total_rows, per_peer,
    mslot, mrow, mmask, fplace, fmask,
    start_ref, blocks_hbm, embed_ref, proj_ref, inverse_ref,
    blocks, own, gathered, partial, narrow_send, narrow_recv, wide_recv, image, line, line_recv,
    load_sem, ag_send, ag_recv, rs_send, rs_recv, ar_send, ar_recv,
):
    bits = devices.bit_length() - 1
    kinds, columns, size = own.shape
    slots = blocks.shape[0]
    wide = wide_recv.shape[0] // kinds
    rows_at = lax.axis_index("rows")
    grp_at = lax.axis_index("grp")
    me = rows_at * 2 + grp_at
    orders = orders_of(bits, kinds)
    places = [place_of(me, order) for order in orders]

    stages = [(0,)] + [tuple(range(b, min(b + 2, bits))) for b in range(1, bits, 2)]
    groups = []
    for stage in stages:
        masks = [1 << stage[0]]
        if len(stage) == 2:
            masks += [1 << stage[1], (1 << stage[0]) + (1 << stage[1])]
        groups.append(masks)
    greeted = sorted(set(sum(groups, [])))

    def partner_of(mask):
        other = me
        for b in range(bits):
            if (mask >> b) % 2:
                other = other + (1 << b) * (1 - 2 * ((me // (1 << b)) % 2))
        return (other // 2, other % 2)

    def partner(b):
        return partner_of(1 << b)

    loads = [
        pltpu.make_async_copy(
            blocks_hbm.at[pl.ds(lo, hi - lo)], blocks.at[pl.ds(lo, hi - lo)], load_sem.at[i]
        )
        for i, (lo, hi) in enumerate(split_even(slots, CHUNKS))
    ]
    for copy in loads:
        copy.start()
    barrier = pltpu.get_barrier_semaphore()
    for mask in greeted:
        pl.semaphore_signal(barrier, inc=1, device_id=partner_of(mask), device_id_type=MESH)
    pl.semaphore_wait(barrier, len(greeted))
    half = devices // 2

    def mirror_sums(device):
        sums = [jnp.zeros((columns, size), jnp.float32) for _ in range(kinds)]
        for j in range(per_peer):
            at = device * per_peer + j
            product = jnp.dot(
                own[mrow[at]], blocks[mslot[at]], preferred_element_type=jnp.float32
            )
            for kind in range(kinds):
                sums[kind] = sums[kind] + product * mmask[kind, at]
        return sums

    def mirror_give(pair, _):
        device = 2 * pair + (1 - grp_at)
        sums = mirror_sums(device)
        for kind in range(kinds):
            at = kind * devices + half + place_of(device, orders[kind]) % half
            narrow_send[at] = sums[kind].astype(jnp.bfloat16)
        return 0

    def mirror_keep(pair, _):
        device = 2 * pair + grp_at
        sums = mirror_sums(device)
        for kind in range(kinds):
            partial[kind * devices + place_of(device, orders[kind])] = sums[kind]
        return 0

    def forward_for(slot, _):
        product = nt_dot(gathered[fplace[slot]], blocks[slot])
        for kind in range(kinds):
            image[kind] = image[kind] + product * fmask[kind, slot]
        return 0

    for iteration in range(ITERS):
        last = iteration == ITERS - 1
        for kind in range(kinds):
            if iteration == 0:
                own[kind] = start_ref[kind]
            gathered[kind * devices + places[kind]] = own[kind]
        image[...] = jnp.zeros_like(image)

        def gather_start(k):
            copies = []
            for kind in range(kinds):
                base = kind * devices + (places[kind] // (1 << k)) * (1 << k)
                span = gathered.at[pl.ds(base, 1 << k)]
                copy = pltpu.make_async_remote_copy(
                    span, span, ag_send.at[kind, k], ag_recv.at[kind, k],
                    device_id=partner(orders[kind][k]), device_id_type=MESH,
                )
                copy.start()
                copies.append(copy)
            return copies

        def gather_wait(copies):
            for copy in copies:
                copy.wait()

        def reduce_start(k):
            count = 1 << k
            copies = []
            for kind in range(kinds):
                place = places[kind]
                give = (
                    kind * devices
                    + (place // (2 * count)) * (2 * count)
                    + (1 - (place // count) % 2) * count
                )
                if k >= bits - NARROW:
                    stage = kind * devices + count

                    def stage_one(i, _, stage=stage, give=give):
                        narrow_send[stage + i] = partial[give + i].astype(jnp.bfloat16)
                        return 0

                    if k < bits - 1:
                        lax.fori_loop(0, count, stage_one, 0)
                    source = narrow_send.at[pl.ds(stage, count)]
                    target = narrow_recv.at[pl.ds(stage, count)]
                else:
                    source = partial.at[pl.ds(give, count)]
                    target = wide_recv.at[pl.ds(kind * wide + count, count)]
                copy = pltpu.make_async_remote_copy(
                    source, target, rs_send.at[kind, k], rs_recv.at[kind, k],
                    device_id=partner(orders[kind][k]), device_id_type=MESH,
                )
                copy.start()
                copies.append(copy)
            return copies

        def reduce_wait(k, copies):
            count = 1 << k
            for kind in range(kinds):
                copies[kind].wait()
                keep = kind * devices + (places[kind] // count) * count

                def add_one(i, _, keep=keep, kind=kind):
                    if k >= bits - NARROW:
                        more = narrow_recv[kind * devices + count + i].astype(jnp.float32)
                    else:
                        more = wide_recv[kind * wide + count + i]
                    partial[keep + i] = partial[keep + i] + more
                    return 0

                lax.fori_loop(0, count, add_one, 0)

        moving = gather_start(0)
        if iteration == 0:
            for copy in loads:
                copy.wait()
        lax.fori_loop(0, half, mirror_give, 0, unroll=2)
        adding = reduce_start(bits - 1)
        lax.fori_loop(0, half // 2, mirror_keep, 0, unroll=2)
        gather_wait(moving)
        moving = gather_start(1)
        lax.fori_loop(half // 2, half, mirror_keep, 0, unroll=2)
        reduce_wait(bits - 1, adding)
        adding = reduce_start(bits - 2)
        for k in range(2, bits):
            gather_wait(moving)
            moving = gather_start(k)
            if k >= 3:
                reduce_wait(bits + 1 - k, adding)
                adding = reduce_start(bits - k)
        gather_wait(moving)
        lax.fori_loop(0, slots // 2, forward_for, 0, unroll=2)
        reduce_wait(1, adding)
        adding = reduce_start(0)
        lax.fori_loop(slots // 2, slots, forward_for, 0, unroll=2)
        reduce_wait(0, adding)

        gram = jnp.zeros((columns, columns), jnp.float32)
        projection = jnp.zeros((columns, columns), jnp.float32)
        for kind in range(kinds):
            rows = image[kind] + partial[kind * devices + places[kind]]
            image[kind] = rows
            gram = gram + nt_dot(rows, rows, HIGH)
            if last:
                projection = projection + nt_dot(own[kind].astype(jnp.float32), rows, HIGH)
        if last:
            tall = columns
            line[0] = jnp.concatenate([gram, projection], axis=1)
        else:
            tall = columns // 2
            line[0, :tall] = jnp.concatenate([gram[:tall], gram[tall:]], axis=1)
        for at, masks in enumerate(groups):
            copies = []
            for j, mask in enumerate(masks):
                copies.append(
                    pltpu.make_async_remote_copy(
                        line.at[at, pl.ds(0, tall)], line_recv.at[at * 3 + j, pl.ds(0, tall)],
                        ar_send.at[at * 3 + j], ar_recv.at[at * 3 + j],
                        device_id=partner_of(mask), device_id_type=MESH,
                    )
                )
            for copy in copies:
                copy.start()
            for copy in copies:
                copy.wait()
            total = line[at, :tall] + line_recv[at * 3, :tall]
            if len(masks) == 3:
                total = total + (line_recv[at * 3 + 1, :tall] + line_recv[at * 3 + 2, :tall])
            line[at + 1, :tall] = total
        whole = line[len(groups), :tall] / total_rows
        if last:
            proj_ref[...] = whole[:, columns:]
        else:
            top = jnp.concatenate([whole[:, :columns], whole[:, columns:]], axis=0)
            whole = jnp.concatenate([top, top], axis=1)
        inverse = inverse_factor(whole, columns)
        if last:
            inverse_ref[...] = inverse
        for kind in range(kinds):
            if last:
                embed_ref[:, kind * size : (kind + 1) * size] = image[kind]
            else:
                result = jnp.dot(
                    inverse, image[kind], precision=HIGH, preferred_element_type=jnp.float32
                )
                own[kind] = result.astype(jnp.bfloat16)


def on_device(start_basis, kernel_blocks, block_row, block_col, block_count):
    devices = lax.axis_size("rows") * lax.axis_size("grp")
    me = lax.axis_index("rows") * lax.axis_size("grp") + lax.axis_index("grp")
    slots, size, _ = kernel_blocks.shape
    own_rows, columns = start_basis.shape
    kinds = own_rows // size
    per_peer = (slots + devices - 1) // devices
    bits = devices.bit_length() - 1
    orders = orders_of(bits, kinds)
    total_rows = own_rows * devices

    positions = jnp.arange(slots, dtype=jnp.int32)
    alive = positions < block_count[0]
    local_row = jnp.clip(block_row - me * kinds, 0, kinds - 1)
    target = block_col // kinds
    target_block = block_col - target * kinds
    earlier = (
        (target[:, None] == target[None, :])
        & alive[None, :]
        & (positions[None, :] < positions[:, None])
    )
    rank = jnp.sum(earlier.astype(jnp.int32), axis=1)
    spot = jnp.where(alive, target * per_peer + rank, -1)
    hit = spot[None, :] == jnp.arange(devices * per_peer, dtype=jnp.int32)[:, None]
    mslot = jnp.sum(jnp.where(hit, positions[None, :], 0), axis=1)
    mrow = jnp.sum(jnp.where(hit, local_row[None, :], 0), axis=1)
    kind_ids = jnp.arange(kinds, dtype=jnp.int32)[:, None]
    mmask = jnp.any(
        hit[None] & (target_block[None, None, :] == kind_ids[:, :, None]), axis=2
    ).astype(jnp.float32)
    fplace = sum(
        jnp.where(target_block == kind, kind * devices + place_of(target, orders[kind]), 0)
        for kind in range(kinds)
    ).astype(jnp.int32)
    fmask = ((local_row[None, :] == kind_ids) & alive[None, :]).astype(jnp.float32)
    start = start_basis.reshape(kinds, size, columns).transpose(0, 2, 1)

    smem = pl.BlockSpec(memory_space=pltpu.SMEM)
    vmem = pl.BlockSpec(memory_space=pltpu.VMEM)
    wide = 1 << max(bits - NARROW, 0)
    image, projected, inverse = pl.pallas_call(
        functools.partial(kernel, devices, total_rows, per_peer),
        out_shape=(
            jax.ShapeDtypeStruct((columns, own_rows), jnp.float32),
            jax.ShapeDtypeStruct((columns, columns), jnp.float32),
            jax.ShapeDtypeStruct((columns, columns), jnp.float32),
        ),
        in_specs=[smem] * 5 + [vmem, pl.BlockSpec(memory_space=pl.ANY)],
        out_specs=(vmem, vmem, vmem),
        scratch_shapes=[
            pltpu.VMEM((slots, size, size), jnp.bfloat16),
            pltpu.VMEM((kinds, columns, size), jnp.bfloat16),
            pltpu.VMEM((kinds * devices, columns, size), jnp.bfloat16),
            pltpu.VMEM((kinds * devices, columns, size), jnp.float32),
            pltpu.VMEM((kinds * devices, columns, size), jnp.bfloat16),
            pltpu.VMEM((kinds * devices, columns, size), jnp.bfloat16),
            pltpu.VMEM((kinds * wide, columns, size), jnp.float32),
            pltpu.VMEM((kinds, columns, size), jnp.float32),
            pltpu.VMEM((bits + 1, columns, 2 * columns), jnp.float32),
            pltpu.VMEM((3 * bits, columns, 2 * columns), jnp.float32),
            pltpu.SemaphoreType.DMA((CHUNKS,)),
            pltpu.SemaphoreType.DMA((kinds, bits)),
            pltpu.SemaphoreType.DMA((kinds, bits)),
            pltpu.SemaphoreType.DMA((kinds, bits)),
            pltpu.SemaphoreType.DMA((kinds, bits)),
            pltpu.SemaphoreType.DMA((3 * bits,)),
            pltpu.SemaphoreType.DMA((3 * bits,)),
        ],
        compiler_params=pltpu.CompilerParams(
            collective_id=0, has_side_effects=True, vmem_limit_bytes=62 * 1024 * 1024
        ),
    )(mslot, mrow, mmask, fplace, fmask, start, kernel_blocks)
    embedded = lax.dot_general(image, inverse, (((0,), (1,)), ((), ())), precision=HIGH)
    return embedded, projected


def solution(mesh):
    in_specs = (
        P(("rows", "grp"), None),
        P(("rows", "grp"), None, None),
        P(("rows", "grp")),
        P(("rows", "grp")),
        P(("rows", "grp")),
    )
    out_specs = (P(("rows", "grp"), None), P())
    return jax.shard_map(
        on_device, mesh=mesh, in_specs=in_specs, out_specs=out_specs, check_vma=False
    )
```

```python
import functools

import jax
import jax.numpy as jnp
from jax import lax
from jax.experimental import pallas as pl
from jax.experimental.pallas import tpu as pltpu
from jax.sharding import PartitionSpec as P

ITERS = 2
MESH = pl.DeviceIdType.MESH
HIGH = lax.Precision.HIGHEST
NARROW = 3
CHUNKS = 4


def orders_of(bits, kinds):
    down = list(range(bits - 1, -1, -1))
    swapped = list(down)
    if bits >= 3:
        swapped[bits - 3], swapped[bits - 2] = swapped[bits - 2], swapped[bits - 3]
    return [down if kind % 2 == 0 else swapped for kind in range(kinds)]


def place_of(device, order):
    return sum(((device // (1 << b)) % 2) * (1 << i) for i, b in enumerate(order))


def split_even(total, parts):
    edges = [total * i // parts for i in range(parts + 1)]
    return list(zip(edges[:-1], edges[1:]))


def nt_dot(a, b, precision=None):
    return lax.dot_general(
        a, b, (((1,), (1,)), ((), ())), preferred_element_type=jnp.float32, precision=precision
    )


def inverse_factor(gram, columns):
    row_id = lax.broadcasted_iota(jnp.int32, (columns, 2 * columns), 0)
    lane_id = lax.broadcasted_iota(jnp.int32, (columns, 2 * columns), 1)
    unit = jnp.where(lane_id == row_id + columns, 1.0, 0.0).astype(jnp.float32)
    work = jnp.where(lane_id < columns, gram, unit)
    for k in range(columns):
        factor = work[:, k : k + 1] * (1.0 / work[k : k + 1, k : k + 1])
        work = jnp.where(row_id > k, work - factor * work[k : k + 1, :], work)
    pivots = jnp.sum(jnp.where(lane_id == row_id, work, 0.0), axis=1, keepdims=True)
    guess = lax.rsqrt(pivots)
    scale = guess * (1.5 - 0.5 * (pivots * guess) * guess)
    return work[:, columns:] * scale


def kernel(
    devices, total_rows, per_peer,
    mslot, mrow, mmask, fplace, fmask,
    start_ref, blocks_hbm, embed_ref, proj_ref, inverse_ref,
    blocks, own, gathered, partial, narrow_send, narrow_recv, wide_recv, image, line, line_recv,
    load_sem, ag_send, ag_recv, rs_send, rs_recv, ar_send, ar_recv,
):
    bits = devices.bit_length() - 1
    kinds, columns, size = own.shape
    slots = blocks.shape[0]
    wide = wide_recv.shape[0] // kinds
    rows_at = lax.axis_index("rows")
    grp_at = lax.axis_index("grp")
    me = rows_at * 2 + grp_at
    orders = orders_of(bits, kinds)
    places = [place_of(me, order) for order in orders]

    stages = [(0,)] + [tuple(range(b, min(b + 2, bits))) for b in range(1, bits, 2)]
    groups = []
    for stage in stages:
        masks = [1 << stage[0]]
        if len(stage) == 2:
            masks += [1 << stage[1], (1 << stage[0]) + (1 << stage[1])]
        groups.append(masks)
    greeted = sorted(set(sum(groups, [])))

    def partner_of(mask):
        other = me
        for b in range(bits):
            if (mask >> b) % 2:
                other = other + (1 << b) * (1 - 2 * ((me // (1 << b)) % 2))
        return (other // 2, other % 2)

    def partner(b):
        return partner_of(1 << b)

    loads = [
        pltpu.make_async_copy(
            blocks_hbm.at[pl.ds(lo, hi - lo)], blocks.at[pl.ds(lo, hi - lo)], load_sem.at[i]
        )
        for i, (lo, hi) in enumerate(split_even(slots, CHUNKS))
    ]
    for copy in loads:
        copy.start()
    barrier = pltpu.get_barrier_semaphore()
    for mask in greeted:
        pl.semaphore_signal(barrier, inc=1, device_id=partner_of(mask), device_id_type=MESH)
    pl.semaphore_wait(barrier, len(greeted))
    half = devices // 2

    def mirror_sums(device):
        sums = [jnp.zeros((columns, size), jnp.float32) for _ in range(kinds)]
        for j in range(per_peer):
            at = device * per_peer + j
            product = jnp.dot(
                own[mrow[at]], blocks[mslot[at]], preferred_element_type=jnp.float32
            )
            for kind in range(kinds):
                sums[kind] = sums[kind] + product * mmask[kind, at]
        return sums

    def mirror_give(pair, _):
        device = 2 * pair + (1 - grp_at)
        sums = mirror_sums(device)
        for kind in range(kinds):
            at = kind * devices + half + place_of(device, orders[kind]) % half
            narrow_send[at] = sums[kind].astype(jnp.bfloat16)
        return 0

    def mirror_keep(pair, _):
        device = 2 * pair + grp_at
        sums = mirror_sums(device)
        for kind in range(kinds):
            partial[kind * devices + place_of(device, orders[kind])] = sums[kind]
        return 0

    def forward_for(slot, _):
        product = nt_dot(gathered[fplace[slot]], blocks[slot])
        for kind in range(kinds):
            image[kind] = image[kind] + product * fmask[kind, slot]
        return 0

    for iteration in range(ITERS):
        last = iteration == ITERS - 1
        for kind in range(kinds):
            if iteration == 0:
                own[kind] = start_ref[kind].astype(jnp.float32).T.astype(jnp.bfloat16)
            gathered[kind * devices + places[kind]] = own[kind]
        image[...] = jnp.zeros_like(image)

        def gather_start(k):
            copies = []
            for kind in range(kinds):
                base = kind * devices + (places[kind] // (1 << k)) * (1 << k)
                span = gathered.at[pl.ds(base, 1 << k)]
                copy = pltpu.make_async_remote_copy(
                    span, span, ag_send.at[kind, k], ag_recv.at[kind, k],
                    device_id=partner(orders[kind][k]), device_id_type=MESH,
                )
                copy.start()
                copies.append(copy)
            return copies

        def gather_wait(copies):
            for copy in copies:
                copy.wait()

        def reduce_start(k):
            count = 1 << k
            copies = []
            for kind in range(kinds):
                place = places[kind]
                give = (
                    kind * devices
                    + (place // (2 * count)) * (2 * count)
                    + (1 - (place // count) % 2) * count
                )
                if k >= bits - NARROW:
                    stage = kind * devices + count

                    def stage_one(i, _, stage=stage, give=give):
                        narrow_send[stage + i] = partial[give + i].astype(jnp.bfloat16)
                        return 0

                    if k < bits - 1:
                        lax.fori_loop(0, count, stage_one, 0)
                    source = narrow_send.at[pl.ds(stage, count)]
                    target = narrow_recv.at[pl.ds(stage, count)]
                else:
                    source = partial.at[pl.ds(give, count)]
                    target = wide_recv.at[pl.ds(kind * wide + count, count)]
                copy = pltpu.make_async_remote_copy(
                    source, target, rs_send.at[kind, k], rs_recv.at[kind, k],
                    device_id=partner(orders[kind][k]), device_id_type=MESH,
                )
                copy.start()
                copies.append(copy)
            return copies

        def reduce_wait(k, copies):
            count = 1 << k
            for kind in range(kinds):
                copies[kind].wait()
                keep = kind * devices + (places[kind] // count) * count

                def add_one(i, _, keep=keep, kind=kind):
                    if k >= bits - NARROW:
                        more = narrow_recv[kind * devices + count + i].astype(jnp.float32)
                    else:
                        more = wide_recv[kind * wide + count + i]
                    partial[keep + i] = partial[keep + i] + more
                    return 0

                lax.fori_loop(0, count, add_one, 0)

        moving = gather_start(0)
        if iteration == 0:
            for copy in loads:
                copy.wait()
        lax.fori_loop(0, half, mirror_give, 0, unroll=4)
        adding = reduce_start(bits - 1)
        lax.fori_loop(0, half // 2, mirror_keep, 0, unroll=4)
        gather_wait(moving)
        moving = gather_start(1)
        lax.fori_loop(half // 2, half, mirror_keep, 0, unroll=4)
        reduce_wait(bits - 1, adding)
        adding = reduce_start(bits - 2)
        for k in range(2, bits):
            gather_wait(moving)
            moving = gather_start(k)
            if k >= 3:
                reduce_wait(bits + 1 - k, adding)
                adding = reduce_start(bits - k)
        gather_wait(moving)
        lax.fori_loop(0, slots // 2, forward_for, 0, unroll=2)
        reduce_wait(1, adding)
        adding = reduce_start(0)
        lax.fori_loop(slots // 2, slots, forward_for, 0, unroll=2)
        reduce_wait(0, adding)

        gram = jnp.zeros((columns, columns), jnp.float32)
        projection = jnp.zeros((columns, columns), jnp.float32)
        for kind in range(kinds):
            rows = image[kind] + partial[kind * devices + places[kind]]
            image[kind] = rows
            gram = gram + nt_dot(rows, rows, HIGH)
            if last:
                projection = projection + nt_dot(own[kind].astype(jnp.float32), rows, HIGH)
        if last:
            tall = columns
            line[0] = jnp.concatenate([gram, projection], axis=1)
        else:
            tall = columns // 2
            line[0, :tall] = jnp.concatenate([gram[:tall], gram[tall:]], axis=1)
        for at, masks in enumerate(groups):
            copies = []
            for j, mask in enumerate(masks):
                copies.append(
                    pltpu.make_async_remote_copy(
                        line.at[at, pl.ds(0, tall)], line_recv.at[at * 3 + j, pl.ds(0, tall)],
                        ar_send.at[at * 3 + j], ar_recv.at[at * 3 + j],
                        device_id=partner_of(mask), device_id_type=MESH,
                    )
                )
            for copy in copies:
                copy.start()
            for copy in copies:
                copy.wait()
            total = line[at, :tall] + line_recv[at * 3, :tall]
            if len(masks) == 3:
                total = total + (line_recv[at * 3 + 1, :tall] + line_recv[at * 3 + 2, :tall])
            line[at + 1, :tall] = total
        whole = line[len(groups), :tall] / total_rows
        if last:
            proj_ref[...] = whole[:, columns:]
        else:
            top = jnp.concatenate([whole[:, :columns], whole[:, columns:]], axis=0)
            whole = jnp.concatenate([top, top], axis=1)
        inverse = inverse_factor(whole, columns)
        if last:
            inverse_ref[...] = inverse
        for kind in range(kinds):
            if last:
                embed_ref[:, kind * size : (kind + 1) * size] = image[kind]
            else:
                result = jnp.dot(
                    inverse, image[kind], precision=HIGH, preferred_element_type=jnp.float32
                )
                own[kind] = result.astype(jnp.bfloat16)


def on_device(start_basis, kernel_blocks, block_row, block_col, block_count):
    devices = lax.axis_size("rows") * lax.axis_size("grp")
    me = lax.axis_index("rows") * lax.axis_size("grp") + lax.axis_index("grp")
    slots, size, _ = kernel_blocks.shape
    own_rows, columns = start_basis.shape
    kinds = own_rows // size
    per_peer = (slots + devices - 1) // devices
    bits = devices.bit_length() - 1
    orders = orders_of(bits, kinds)
    total_rows = own_rows * devices

    positions = jnp.arange(slots, dtype=jnp.int32)
    alive = positions < block_count[0]
    local_row = jnp.clip(block_row - me * kinds, 0, kinds - 1)
    target = block_col // kinds
    target_block = block_col - target * kinds
    earlier = (
        (target[:, None] == target[None, :])
        & alive[None, :]
        & (positions[None, :] < positions[:, None])
    )
    rank = jnp.sum(earlier.astype(jnp.int32), axis=1)
    spot = jnp.where(alive, target * per_peer + rank, -1)
    hit = spot[None, :] == jnp.arange(devices * per_peer, dtype=jnp.int32)[:, None]
    mslot = jnp.sum(jnp.where(hit, positions[None, :], 0), axis=1)
    mrow = jnp.sum(jnp.where(hit, local_row[None, :], 0), axis=1)
    kind_ids = jnp.arange(kinds, dtype=jnp.int32)[:, None]
    mmask = jnp.any(
        hit[None] & (target_block[None, None, :] == kind_ids[:, :, None]), axis=2
    ).astype(jnp.float32)
    fplace = sum(
        jnp.where(target_block == kind, kind * devices + place_of(target, orders[kind]), 0)
        for kind in range(kinds)
    ).astype(jnp.int32)
    fmask = ((local_row[None, :] == kind_ids) & alive[None, :]).astype(jnp.float32)
    start = start_basis.reshape(kinds, size, columns)

    smem = pl.BlockSpec(memory_space=pltpu.SMEM)
    vmem = pl.BlockSpec(memory_space=pltpu.VMEM)
    wide = 1 << max(bits - NARROW, 0)
    image, projected, inverse = pl.pallas_call(
        functools.partial(kernel, devices, total_rows, per_peer),
        out_shape=(
            jax.ShapeDtypeStruct((columns, own_rows), jnp.float32),
            jax.ShapeDtypeStruct((columns, columns), jnp.float32),
            jax.ShapeDtypeStruct((columns, columns), jnp.float32),
        ),
        in_specs=[smem] * 5 + [vmem, pl.BlockSpec(memory_space=pl.ANY)],
        out_specs=(vmem, vmem, vmem),
        scratch_shapes=[
            pltpu.VMEM((slots, size, size), jnp.bfloat16),
            pltpu.VMEM((kinds, columns, size), jnp.bfloat16),
            pltpu.VMEM((kinds * devices, columns, size), jnp.bfloat16),
            pltpu.VMEM((kinds * devices, columns, size), jnp.float32),
            pltpu.VMEM((kinds * devices, columns, size), jnp.bfloat16),
            pltpu.VMEM((kinds * devices, columns, size), jnp.bfloat16),
            pltpu.VMEM((kinds * wide, columns, size), jnp.float32),
            pltpu.VMEM((kinds, columns, size), jnp.float32),
            pltpu.VMEM((bits + 1, columns, 2 * columns), jnp.float32),
            pltpu.VMEM((3 * bits, columns, 2 * columns), jnp.float32),
            pltpu.SemaphoreType.DMA((CHUNKS,)),
            pltpu.SemaphoreType.DMA((kinds, bits)),
            pltpu.SemaphoreType.DMA((kinds, bits)),
            pltpu.SemaphoreType.DMA((kinds, bits)),
            pltpu.SemaphoreType.DMA((kinds, bits)),
            pltpu.SemaphoreType.DMA((3 * bits,)),
            pltpu.SemaphoreType.DMA((3 * bits,)),
        ],
        compiler_params=pltpu.CompilerParams(
            collective_id=0, has_side_effects=True, vmem_limit_bytes=62 * 1024 * 1024
        ),
    )(mslot, mrow, mmask, fplace, fmask, start, kernel_blocks)
    embedded = lax.dot_general(image, inverse, (((0,), (1,)), ((), ())), precision=HIGH)
    return embedded, projected


def solution(mesh):
    in_specs = (
        P(("rows", "grp"), None),
        P(("rows", "grp"), None, None),
        P(("rows", "grp")),
        P(("rows", "grp")),
        P(("rows", "grp")),
    )
    out_specs = (P(("rows", "grp"), None), P())
    return jax.shard_map(
        on_device, mesh=mesh, in_specs=in_specs, out_specs=out_specs, check_vma=False
    )
```
